256 devices in a mesh: gx: 32 (over x, y, core), gy: 8 (over z).
Axes of the slice: x: 4, y: 4, z: 8, core: 2. Of those that a mesh axis runs over, the one named last changes fastest.
Arguments:
- u_vel: bfloat16 [128, 1024, 2048], P(None, 'gx', 'gy'), may hold values from -6 to 6
- v_vel: bfloat16 [128, 1024, 2048], P(None, 'gx', 'gy'), may hold values from -6 to 6
- inv_dx: float32 [1024, 2048], P('gx', 'gy'), may hold values from 0.5 to 2
- inv_dy: float32 [1024, 2048], P('gx', 'gy'), may hold values from 0.5 to 2
Outputs:
- recon_vorticity: bfloat16 [128, 1024, 2048], P(None, 'gx', 'gy')
- recon_divergence: bfloat16 [128, 1024, 2048], P(None, 'gx', 'gy')
The draws below stay inside these ranges and needn't reach their ends.
All inputs are finite; a program needn't handle non-finite values.
Results may differ from the reference program's by a relative error of at most 0.0045.
Values may be sent and summed in bfloat16 or wider, within the bound.
No kernel may reach another device: no remote copies, remote signals or barrier semaphores. Data moves between devices by JAX's collectives and lax.ppermute only.
A program may use at most 64 MiB of HBM per device.

```python
import math
import jax
import jax.numpy as jnp
from jax import lax

M = 128
CX = 32
ITERS = 8
NX = 1024
NY = 2048
N_GX = 32


def velocity_field(key):
    mode_count = 24
    keys = jax.random.split(key, 10)
    across = (jnp.arange(NX, dtype=jnp.float32) + 0.5) / NX
    upward = (jnp.arange(NY, dtype=jnp.float32) + 0.5) / NY
    trend = jnp.power(3.0, 0.5 * across)[:, None] * jnp.power(3.0, 0.5 * upward)[None, :]
    center_x = jax.random.uniform(keys[0], (mode_count,), jnp.float32, 0.0, 1.0)
    center_y = jax.random.uniform(keys[1], (mode_count,), jnp.float32, 0.0, 1.0)
    width_x = jax.random.uniform(keys[2], (mode_count,), jnp.float32, 0.12, 0.45)
    width_y = jax.random.uniform(keys[3], (mode_count,), jnp.float32, 0.12, 0.45)
    height = jnp.exp(jax.random.uniform(keys[4], (mode_count,), jnp.float32, math.log(0.15), math.log(0.8)))
    frequency = jnp.exp(jax.random.uniform(keys[5], (mode_count, 2), jnp.float32, math.log(0.5), math.log(24.0)))
    phase = jax.random.uniform(keys[6], (mode_count, 2), jnp.float32, -math.pi, math.pi)
    ratio = jax.random.uniform(keys[7], (mode_count,), jnp.float32, 0.0, 0.8)
    moments = jnp.arange(M, dtype=jnp.float32)
    total = jnp.zeros((M, NX, NY), jnp.float32)
    for mode in range(mode_count):
        rough = jax.random.uniform(jax.random.fold_in(keys[8], mode), (NX, NY), jnp.float32, 0.5, 1.5)
        bump_x = jnp.exp(-jnp.square((across - center_x[mode]) / width_x[mode]))
        bump_y = jnp.exp(-jnp.square((upward - center_y[mode]) / width_y[mode]))
        envelope = height[mode] * bump_x[:, None] * bump_y[None, :] * rough
        temporal = jnp.cos(2.0 * math.pi * frequency[mode, 0] * moments / M + phase[mode, 0])
        temporal = temporal + ratio[mode] * jnp.cos(2.0 * math.pi * frequency[mode, 1] * moments / M + phase[mode, 1])
        total = total + temporal[:, None, None] * envelope[None]
    signal = total * trend[None]
    noise = jnp.clip(0.3 * jax.random.normal(keys[9], (M, NX, NY), jnp.float32), -1.2, 1.2)
    return jnp.clip(signal + noise, -6.0, 6.0)


def draw_u_vel(key, part):
    return velocity_field(jax.random.fold_in(key, 11)).astype(jnp.bfloat16)


def draw_v_vel(key, part):
    return velocity_field(jax.random.fold_in(key, 23)).astype(jnp.bfloat16)


def shard_levels(rng, extent, cuts, low, top_value):
    level = 1.0
    for position, shards_of in cuts:
        steps = jax.random.uniform(jax.random.fold_in(jax.random.fold_in(rng, 6), position), (shards_of,), jnp.float32, low / len(cuts), top_value / len(cuts))
        level = level * jnp.repeat(jnp.exp(steps), extent[position] // shards_of).reshape((-1,) + (1,) * (len(extent) - 1 - position))
    return level


def setup_inputs(seed: int = 0) -> dict:
    key_of = jax.random.split(jax.random.key(seed), 5)
    return {
        "u_vel": draw_u_vel(jax.random.fold_in(key_of[4], 71), 0),
        "v_vel": draw_v_vel(jax.random.fold_in(key_of[4], 71), 0),
        "inv_dx": jnp.clip(jnp.exp(math.log(2.0) - 1.3862944 * jax.random.uniform(key_of[2], (NX, NY), jnp.float32) ** shard_levels(key_of[2], (NX, NY), ((0, 32), (1, 8)), -0.2, 0.2)), 0.5, 2.0),
        "inv_dy": jnp.clip(jnp.exp(math.log(2.0) - 1.3862944 * jax.random.uniform(key_of[3], (NX, NY), jnp.float32) ** shard_levels(key_of[3], (NX, NY), ((0, 32), (1, 8)), -0.2, 0.2)), 0.5, 2.0),
    }


def along_first(padded):
    return (padded[..., 0:-4, 2:-2] - 8.0 * padded[..., 1:-3, 2:-2] + 8.0 * padded[..., 3:-1, 2:-2] - padded[..., 4:, 2:-2]) / 12.0

def along_second(padded):
    return (padded[..., 2:-2, 0:-4] - 8.0 * padded[..., 2:-2, 1:-3] + 8.0 * padded[..., 2:-2, 3:-1] - padded[..., 2:-2, 4:]) / 12.0

def spectral_filter(gram_sum):
    order = gram_sum.shape[0]
    identity = jnp.eye(order, dtype=jnp.float32)
    shift = jnp.trace(gram_sum) / order
    scale = jnp.sqrt(jnp.sum(gram_sum * gram_sum))
    signum = (gram_sum - shift * identity) / scale
    for sweep in range(ITERS):
        square = jnp.dot(signum, signum, precision=lax.Precision.HIGHEST)
        cube = jnp.dot(signum, square, precision=lax.Precision.HIGHEST)
        signum = 1.5 * signum - 0.5 * cube
    return ((identity + signum) * 0.5).astype(jnp.bfloat16)

def reference(u_vel, v_vel, inv_dx, inv_dy):

    def snapshot_fields(pair):
        pad_u = jnp.pad(pair[0].astype(jnp.float32), 2)
        pad_v = jnp.pad(pair[1].astype(jnp.float32), 2)
        vorticity = (inv_dx * along_first(pad_v) - inv_dy * along_second(pad_u)).astype(jnp.bfloat16)
        divergence = (inv_dx * along_first(pad_u) + inv_dy * along_second(pad_v)).astype(jnp.bfloat16)
        return (vorticity, divergence)
    vorticity, divergence = lax.map(snapshot_fields, (u_vel, v_vel))
    stacked = jnp.concatenate([vorticity, divergence], 0)
    order = 2 * M

    def add_block(block_index, gram_sum):
        start = (block_index * CX).astype(jnp.int32)
        block = lax.dynamic_slice_in_dim(stacked, start, CX, 1).reshape(order, CX * NY).astype(jnp.float32)
        return gram_sum + jnp.dot(block, block.T, precision=lax.Precision.HIGHEST)
    gram_sum = lax.fori_loop(0, N_GX, add_block, jnp.zeros((order, order), jnp.float32))
    filter_bf = spectral_filter(gram_sum)
    filter_tr = filter_bf.T.astype(jnp.float32)

    def rebuild(block_index):
        start = (block_index * CX).astype(jnp.int32)
        block = lax.dynamic_slice_in_dim(stacked, start, CX, 1).reshape(order, CX * NY).astype(jnp.float32)
        mixed = jnp.dot(filter_tr, block, precision=lax.Precision.HIGHEST)
        return mixed.astype(jnp.bfloat16).reshape(order, CX, NY)
    pieces = lax.map(rebuild, jnp.arange(N_GX).astype(jnp.int32))
    rebuilt = jnp.transpose(pieces, (1, 0, 2, 3)).reshape(order, NX, NY)
    return (rebuilt[:M], rebuilt[M:])
```

```python
import functools

import jax
import jax.numpy as jnp
from jax import lax
from jax.experimental import pallas as pl
from jax.experimental.pallas import tpu as pltpu
from jax.sharding import PartitionSpec as P

ITERS = 8
TB = 16
HALF_ROWS = 136


f32 = jnp.float32
bf16 = jnp.bfloat16


def iotas(rows, cols):
    r = lax.broadcasted_iota(jnp.int32, (rows, cols), 0)
    c = lax.broadcasted_iota(jnp.int32, (rows, cols), 1)
    return r, c


def swap_matrix():
    r, c = iotas(256, 256)
    return jnp.where(c == ((r & 15) << 4) + (r >> 4), 1.0, 0.0).astype(bf16)


def relayout_kernel(u_ref, v_ref, uv_ref, ylow_ref, yhigh_ref, xlow_ref, xhigh_ref, swap):
    @pl.when(pl.program_id(0) == 0)
    def _():
        swap[...] = swap_matrix()

    p = swap[...]
    _, lane = iotas(TB, 128)
    low = jnp.zeros((TB, 128), f32)
    high = jnp.zeros((TB, 128), f32)
    for f, ref in enumerate((u_ref, v_ref)):
        for h in range(2):
            block = ref[:, 16 * h : 16 * h + 16, :].reshape(256, 256)
            rows = jnp.dot(p, block, preferred_element_type=f32)
            uv_ref[16 * h : 16 * h + 16, f] = rows.astype(bf16).reshape(16, TB, 256)
            for k in range(16):
                at = 64 * f + 2 * (16 * h + k)
                left = rows[TB * k : TB * k + TB, 0:128]
                right = rows[TB * k : TB * k + TB, 128:256]
                here = (lane >> 1) == (at >> 1)
                left = pltpu.roll(left, at, axis=1) if at else left
                right = pltpu.roll(right, (at + 2) % 128, axis=1) if (at + 2) % 128 else right
                low = jnp.where(here, left, low)
                high = jnp.where(here, right, high)
    ylow_ref[...] = low.astype(bf16)
    yhigh_ref[...] = high.astype(bf16)
    for f in range(2):
        for k in range(2):
            xlow_ref[k, f] = uv_ref[k, f]
            xhigh_ref[k, f] = uv_ref[30 + k, f]


def relayout(u, v):
    snaps, tile_x, tile_y = u.shape
    steps = snaps // TB
    return pl.pallas_call(
        relayout_kernel,
        grid=(steps,),
        in_specs=[pl.BlockSpec((TB, tile_x, tile_y), lambda i: (i, 0, 0))] * 2,
        out_specs=[
            pl.BlockSpec((tile_x, 2, TB, tile_y), lambda i: (0, 0, i, 0)),
            pl.BlockSpec((TB, 128), lambda i: (i, 0)),
            pl.BlockSpec((TB, 128), lambda i: (i, 0)),
            pl.BlockSpec((2, 2, TB, tile_y), lambda i: (0, 0, i, 0)),
            pl.BlockSpec((2, 2, TB, tile_y), lambda i: (0, 0, i, 0)),
        ],
        out_shape=[
            jax.ShapeDtypeStruct((tile_x, 2, snaps, tile_y), bf16),
            jax.ShapeDtypeStruct((snaps, 128), bf16),
            jax.ShapeDtypeStruct((snaps, 128), bf16),
            jax.ShapeDtypeStruct((2, 2, snaps, tile_y), bf16),
            jax.ShapeDtypeStruct((2, 2, snaps, tile_y), bf16),
        ],
        scratch_shapes=[pltpu.VMEM((256, 256), bf16)],
        name="relayout",
    )(u, v)


XB = 4


def stencil_kernel(
    core_ref, uv_hbm, xlow_hbm, xhigh_hbm, ylow_ref, yhigh_ref, idx_ref, idy_ref,
    s_ref, keep_ref, give_ref,
    uv, band, edge, gram, sems,
):
    i = pl.program_id(0)
    n = pl.num_programs(0)

    def chunk(k):
        return pltpu.make_async_copy(
            uv_hbm.at[pl.ds(XB * k, XB)], uv.at[pl.ds(2 + XB * k, XB)], sems.at[k]
        )

    lows = pltpu.make_async_copy(xlow_hbm, uv.at[pl.ds(0, 2)], sems.at[8])
    highs = pltpu.make_async_copy(xhigh_hbm, uv.at[pl.ds(34, 2)], sems.at[9])

    @pl.when(i == 0)
    def _():
        lows.start()
        for k in range(8):
            chunk(k).start()
        highs.start()
        gram[...] = jnp.zeros_like(gram)
        r, c = iotas(256, 256)
        d = c - r
        band[...] = (
            jnp.where(d == 2, 1.0, 0.0) - jnp.where(d == 1, 8.0, 0.0)
            + jnp.where(d == -1, 8.0, 0.0) - jnp.where(d == -2, 1.0, 0.0)
        ).astype(bf16)
        r, c = iotas(128, 128)
        for f in range(2):
            pair = (r - 64 * f) >> 1
            mine = pair == (c >> 2)
            k = r & 1
            j = c & 3
            from_low = jnp.where(
                mine & (j == 2), jnp.where(k == 0, 1.0, -8.0),
                jnp.where(mine & (j == 3) & (k == 1), 1.0, 0.0),
            ).astype(bf16)
            from_high = jnp.where(
                mine & (j == 1), jnp.where(k == 0, 8.0, -1.0),
                jnp.where(mine & (j == 0) & (k == 0), -1.0, 0.0),
            ).astype(bf16)
            edge[128 * f : 128 * f + 128, :] = jnp.dot(
                ylow_ref[...], from_low, preferred_element_type=f32
            ) + jnp.dot(yhigh_ref[...], from_high, preferred_element_type=f32)
        lows.wait()
        chunk(0).wait()

    @pl.when(i < n - 1)
    def _():
        chunk(i + 1).wait()

    @pl.when(i == n - 1)
    def _():
        highs.wait()

    _, lane = iotas(256, 128)
    parts = []
    for j in range(XB):
        x = XB * i + j
        rows = uv[x + 2].reshape(256, 256)
        dy = jnp.dot(rows, band[...], preferred_element_type=f32)
        turned = pltpu.roll(edge[...], 126 - 4 * x, axis=1)
        dy = jnp.concatenate(
            [
                dy[:, 0:128] + jnp.where(lane < 2, turned, 0.0),
                dy[:, 128:256] + jnp.where(lane >= 126, turned, 0.0),
            ],
            axis=1,
        )
        a = uv[x].reshape(256, 256).astype(f32)
        b = uv[x + 1].reshape(256, 256).astype(f32)
        c = uv[x + 3].reshape(256, 256).astype(f32)
        d = uv[x + 4].reshape(256, 256).astype(f32)
        dx = 8.0 * (c - b) + (a - d)
        inv_x = idx_ref[pl.ds(x, 1), :] * (1.0 / 12.0)
        inv_y = idy_ref[pl.ds(x, 1), :] * (1.0 / 12.0)
        vort = (inv_x * dx[128:256] - inv_y * dy[0:128]).astype(bf16)
        div = (inv_x * dx[0:128] + inv_y * dy[128:256]).astype(bf16)
        s_ref[j, 0:128] = vort
        s_ref[j, 128:256] = div
        parts.append(jnp.concatenate([vort, div], axis=0))
    cells = jnp.concatenate(parts, axis=1)
    gram[...] += lax.dot_general(
        cells, cells, (((1,), (1,)), ((), ())), preferred_element_type=f32
    )

    @pl.when(i == n - 1)
    def _():
        r, c = iotas(128, 128)
        dd = gram[128:256, 128:256]
        mixed = jnp.where(r <= c, gram[0:128, 0:128], dd)
        diag = jnp.sum(jnp.where(r == c, dd, 0.0), axis=0, keepdims=True)
        diag = jnp.broadcast_to(diag, (8, 128))
        first = core_ref[0] == 0
        cross = gram[0:128, 128:256]
        keep_ref[0:128] = jnp.where(first, cross, mixed)
        give_ref[0:128] = jnp.where(first, mixed, cross)
        keep_ref[128:136] = jnp.where(first, 0.0, diag)
        give_ref[128:136] = jnp.where(first, diag, 0.0)


def stencil(core, uv, xlow, xhigh, ylow, yhigh, inv_dx, inv_dy):
    tile_x, _, snaps, tile_y = uv.shape
    vmem = pl.BlockSpec(memory_space=pltpu.VMEM)
    whole = pl.BlockSpec(memory_space=pl.ANY)
    half = jax.ShapeDtypeStruct((HALF_ROWS, 128), f32)
    return pl.pallas_call(
        stencil_kernel,
        grid=(tile_x // XB,),
        in_specs=[pl.BlockSpec(memory_space=pltpu.SMEM), whole, whole, whole, vmem, vmem, vmem, vmem],
        out_specs=[
            pl.BlockSpec((XB, 2 * snaps, tile_y), lambda i: (i, 0, 0)),
            pl.BlockSpec((HALF_ROWS, 128), lambda i: (0, 0)),
            pl.BlockSpec((HALF_ROWS, 128), lambda i: (0, 0)),
        ],
        out_shape=[jax.ShapeDtypeStruct((tile_x, 2 * snaps, tile_y), bf16), half, half],
        scratch_shapes=[
            pltpu.VMEM((36, 2, 128, 256), bf16),
            pltpu.VMEM((256, 256), bf16),
            pltpu.VMEM((256, 128), f32),
            pltpu.VMEM((256, 256), f32),
            pltpu.SemaphoreType.DMA((10,)),
        ],
        name="stencil",
    )(core, uv, xlow, xhigh, ylow, yhigh, inv_dx, inv_dy)


def split(a):
    hi = a.astype(bf16)
    return hi, (a - hi.astype(f32)).astype(bf16)


def product(a, b):
    (ah, al), (bh, bl) = a, b
    left = jnp.concatenate([ah, ah, al], axis=1)
    right = jnp.concatenate([bh, bl, bh], axis=0)
    return jnp.dot(left, right, preferred_element_type=f32)


def rebuild_kernel(core_ref, mine_ref, other_ref, s_hbm, vort_ref, div_ref, s, filt, swap, mixed, sems):
    i = pl.program_id(0)

    def chunk(k):
        return pltpu.make_async_copy(s_hbm.at[pl.ds(16 * k, 16)], s.at[pl.ds(16 * k, 16)], sems.at[k])

    @pl.when(i == 0)
    def _():
        chunk(0).start()
        chunk(1).start()
        swap[...] = swap_matrix()
        first = core_ref[0] == 0
        cross = jnp.where(first, mine_ref[0:128], other_ref[0:128])
        both = jnp.where(first, other_ref[0:128], mine_ref[0:128])
        diag = jnp.where(first, other_ref[128:136], mine_ref[128:136])[0:1]
        r, c = iotas(128, 128)
        turned = both.T
        vv = jnp.where(r <= c, both, turned)
        dd = jnp.where(r == c, diag, jnp.where(r > c, both, turned))
        gram = jnp.concatenate(
            [jnp.concatenate([vv, cross], axis=1), jnp.concatenate([cross.T, dd], axis=1)], axis=0
        )
        r, c = iotas(256, 256)
        eye = jnp.where(r == c, 1.0, 0.0)
        shift = jnp.sum(gram * eye, keepdims=True) * (1.0 / 256.0)
        scale = jnp.sqrt(jnp.sum(gram * gram, keepdims=True))
        signum = (gram - shift * eye) / scale
        for _ in range(ITERS):
            parts = split(signum)
            square = product(parts, parts)
            cube = product(parts, split(square))
            signum = 1.5 * signum - 0.5 * cube
        filt[...] = ((eye + signum) * 0.5).astype(bf16)
        chunk(0).wait()

    @pl.when(i == 1)
    def _():
        chunk(1).wait()

    weights = filt[...]
    for k in range(16):
        mixed[k] = jnp.dot(weights, s[16 * i + k], preferred_element_type=f32).astype(bf16)
    p = swap[...]
    for k in range(16):
        block = mixed[:, 16 * k : 16 * k + 16, :].reshape(256, 256)
        rows = jnp.dot(p, block, preferred_element_type=f32).astype(bf16).reshape(16, 16, 256)
        if k < 8:
            vort_ref[16 * k : 16 * k + 16] = rows
        else:
            div_ref[16 * k - 128 : 16 * k - 112] = rows


def rebuild(core, mine, other, s):
    tile_x, rows, tile_y = s.shape
    vmem = pl.BlockSpec(memory_space=pltpu.VMEM)
    out = pl.BlockSpec((128, 16, tile_y), lambda i: (0, i, 0))
    shape = jax.ShapeDtypeStruct((128, tile_x, tile_y), bf16)
    return pl.pallas_call(
        rebuild_kernel,
        grid=(2,),
        in_specs=[pl.BlockSpec(memory_space=pltpu.SMEM), vmem, vmem, pl.BlockSpec(memory_space=pl.ANY)],
        out_specs=[out, out],
        out_shape=[shape, shape],
        scratch_shapes=[
            pltpu.VMEM((tile_x, rows, tile_y), bf16),
            pltpu.VMEM((256, 256), bf16),
            pltpu.VMEM((256, 256), bf16),
            pltpu.VMEM((16, 256, 256), bf16),
            pltpu.SemaphoreType.DMA((2,)),
        ],
        name="rebuild",
    )(core, mine, other, s)


def moved(block, axis, target):
    return lax.ppermute(block, axis, [(i, target(i)) for i in range(lax.axis_size(axis))])


def digit(low, count, by):
    def target(i):
        at = i // low % count
        return i + ((at + by) % count - at) * low

    return target


def gathered_sum(block, axis, low, count):
    others = [moved(block, axis, digit(low, count, by)) for by in range(1, count)]
    for other in others:
        block = block + other
    return block


def per_device(u_vel, v_vel, inv_dx, inv_dy):
    uv, ylow, yhigh, xlow, xhigh = relayout(u_vel, v_vel)

    def shifted(block, axis, step):
        count = lax.axis_size(axis)
        return lax.ppermute(block, axis, [(i, i + step) for i in range(count) if 0 <= i + step < count])

    from_low = shifted(xhigh, "gx", 1)
    from_high = shifted(xlow, "gx", -1)
    from_left = shifted(yhigh, "gy", 1)
    from_right = shifted(ylow, "gy", -1)
    core = jnp.reshape(lax.axis_index("gx") & 1, (1,)).astype(jnp.int32)
    s, keep, give = stencil(core, uv, from_low, from_high, from_left, from_right, inv_dx, inv_dy)
    part = keep + moved(give, "gx", digit(1, 2, 1))
    part = gathered_sum(part, "gx", 2, 4)
    part = gathered_sum(part, "gx", 8, 4)
    part = gathered_sum(part, "gy", 1, 2)
    part = gathered_sum(part, "gy", 2, 4)
    other = moved(part, "gx", digit(1, 2, 1))
    return tuple(rebuild(core, part, other, s))


def solution(mesh):
    in_specs = (P(None, "gx", "gy"), P(None, "gx", "gy"), P("gx", "gy"), P("gx", "gy"))
    out_specs = (P(None, "gx", "gy"), P(None, "gx", "gy"))
    return jax.shard_map(
        per_device, mesh=mesh, in_specs=in_specs, out_specs=out_specs, check_vma=False
    )
```

```python
import functools

import jax
import jax.numpy as jnp
from jax import lax
from jax.experimental import pallas as pl
from jax.experimental.pallas import tpu as pltpu
from jax.sharding import PartitionSpec as P

ITERS = 8
TB = 16
HALF_ROWS = 136


f32 = jnp.float32
bf16 = jnp.bfloat16


def iotas(rows, cols):
    r = lax.broadcasted_iota(jnp.int32, (rows, cols), 0)
    c = lax.broadcasted_iota(jnp.int32, (rows, cols), 1)
    return r, c


def swap_matrix():
    r, c = iotas(256, 256)
    return jnp.where(c == ((r & 15) << 4) + (r >> 4), 1.0, 0.0).astype(bf16)


def relayout_kernel(core_ref, u_hbm, v_hbm, rows_ref, wide_ref, ends_ref, xlow_ref, xhigh_ref, u, v, swap, sems):
    def chunk(k, f):
        at = pl.ds(TB * k, TB)
        return pltpu.make_async_copy((u_hbm, v_hbm)[f].at[at], (u, v)[f].at[at], sems.at[k, f])

    for k in range(8):
        for f in range(2):
            chunk(k, f).start()
    swap[...] = swap_matrix()
    _, lane = iotas(TB, 128)

    @pl.loop(0, 8)
    def _(i):
        at = pl.ds(pl.multiple_of(TB * i, TB), TB)
        p = swap[...]
        for f, tile in enumerate((u, v)):
            chunk(i, f).wait()
            ends = jnp.zeros((TB, 128), f32)
            for h in range(2):
                block = tile[at, 16 * h : 16 * h + 16, :].reshape(256, 256)
                rows = jnp.dot(p, block, preferred_element_type=f32)
                rows_ref[16 * h : 16 * h + 16, f, at] = rows.astype(bf16).reshape(16, TB, 256)
                wide_ref[16 * h : 16 * h + 16, f, at] = rows.reshape(16, TB, 256)
                for k in range(16):
                    x = 16 * h + k
                    part = rows[TB * k : TB * k + TB]
                    part = jnp.where(lane < 64, part[:, 0:128], part[:, 128:256])
                    part = pltpu.roll(part, (4 * x + 2) % 128, axis=1)
                    ends = jnp.where((lane >> 2) == x, part, ends)
            ends_ref[at, 128 * f : 128 * f + 128] = ends.astype(bf16)

    for k in range(2):
        xlow_ref[k] = rows_ref[k]
        xhigh_ref[k] = rows_ref[30 + k]


def relayout(core, u, v):
    snaps, tile_x, tile_y = u.shape
    vmem = pl.BlockSpec(memory_space=pltpu.VMEM)
    whole = pl.BlockSpec(memory_space=pltpu.HBM)
    return pl.pallas_call(
        relayout_kernel,
        in_specs=[pl.BlockSpec(memory_space=pltpu.SMEM), whole, whole],
        out_specs=[vmem] * 5,
        out_shape=[
            pltpu.VMEM((tile_x, 2, snaps, tile_y), bf16),
            pltpu.VMEM((tile_x, 2, snaps, tile_y), f32),
            pltpu.VMEM((snaps, 256), bf16),
            pltpu.VMEM((2, 2, snaps, tile_y), bf16),
            pltpu.VMEM((2, 2, snaps, tile_y), bf16),
        ],
        scratch_shapes=[
            pltpu.VMEM((snaps, tile_x, tile_y), bf16),
            pltpu.VMEM((snaps, tile_x, tile_y), bf16),
            pltpu.VMEM((256, 256), bf16),
            pltpu.SemaphoreType.DMA((8, 2)),
        ],
        compiler_params=pltpu.CompilerParams(vmem_limit_bytes=50 * 2**20),
        name="relayout",
    )(core, u, v)


XB = 4


def stencil_kernel(
    core_ref, rows_ref, wide_ref, xlow_ref, xhigh_ref, left_ref, right_ref, idx_ref, idy_ref,
    s_ref, keep_ref, give_ref,
    band, ends, tall, gram,
):
    r, c = iotas(256, 256)
    d = c - r
    band[...] = (
        jnp.where(d == 2, 1.0, 0.0) - jnp.where(d == 1, 8.0, 0.0)
        + jnp.where(d == -1, 8.0, 0.0) - jnp.where(d == -2, 1.0, 0.0)
    ).astype(bf16)
    _, lane = iotas(128, 128)
    for f in range(2):
        at = slice(128 * f, 128 * f + 128)
        ends[at] = jnp.where(
            (lane & 3) < 2, left_ref[:, at].astype(f32), right_ref[:, at].astype(f32)
        ).astype(bf16)
    r, c = iotas(240, 256)
    for j in range(XB):
        m = r - (112 + 4 * j)
        tall[j] = (
            jnp.where(((m == 0) & (c == 0)) | ((m == 1) & (c == 1)), 1.0, 0.0)
            - jnp.where((m == 1) & (c == 0), 8.0, 0.0)
            + jnp.where((m == 2) & (c == 255), 8.0, 0.0)
            - jnp.where(((m == 2) & (c == 254)) | ((m == 3) & (c == 255)), 1.0, 0.0)
        ).astype(bf16)
    gram[...] = jnp.zeros_like(gram)

    def wide(x):
        if isinstance(x, int) and x < 0:
            return xlow_ref[x + 2].reshape(256, 256).astype(f32)
        if isinstance(x, int) and x >= 32:
            return xhigh_ref[x - 32].reshape(256, 256).astype(f32)
        return wide_ref[x].reshape(256, 256)

    def group(g):
        parts = []
        start = 112 - 16 * g
        if not isinstance(g, int):
            start = pl.multiple_of(start, 16)
        for j in range(XB):
            x = XB * g + j
            dy = jnp.dot(
                jnp.concatenate([rows_ref[x].reshape(256, 256), ends[...]], axis=1),
                jnp.concatenate([band[...], tall[j, pl.ds(start, 128)]], axis=0),
                preferred_element_type=f32,
            )
            dx = 8.0 * (wide(x + 1) - wide(x - 1)) + (wide(x - 2) - wide(x + 2))
            inv_x = idx_ref[pl.ds(x, 1), :] * (1.0 / 12.0)
            inv_y = idy_ref[pl.ds(x, 1), :] * (1.0 / 12.0)
            vort = (inv_x * dx[128:256] - inv_y * dy[0:128]).astype(bf16)
            div = (inv_x * dx[0:128] + inv_y * dy[128:256]).astype(bf16)
            both = jnp.concatenate([vort, div], axis=0)
            s_ref[x] = both
            parts.append(both)
        cells = jnp.concatenate(parts, axis=1)
        gram[...] += lax.dot_general(
            cells, cells, (((1,), (1,)), ((), ())), preferred_element_type=f32
        )

    group(0)

    @pl.loop(1, 7)
    def _(g):
        group(g)

    group(7)

    r, c = iotas(128, 128)
    dd = gram[128:256, 128:256]
    mixed = jnp.where(r <= c, gram[0:128, 0:128], dd)
    diag = jnp.sum(jnp.where(r == c, dd, 0.0), axis=0, keepdims=True)
    diag = jnp.broadcast_to(diag, (8, 128))
    first = core_ref[0] == 0
    cross = gram[0:128, 128:256]
    keep_ref[0:128] = jnp.where(first, cross, mixed)
    give_ref[0:128] = jnp.where(first, mixed, cross)
    keep_ref[128:136] = jnp.where(first, 0.0, diag)
    give_ref[128:136] = jnp.where(first, diag, 0.0)


def stencil(core, rows, wide, xlow, xhigh, left, right, inv_dx, inv_dy):
    tile_x, _, snaps, tile_y = rows.shape
    vmem = pl.BlockSpec(memory_space=pltpu.VMEM)
    half = pltpu.VMEM((HALF_ROWS, 128), f32)
    return pl.pallas_call(
        stencil_kernel,
        in_specs=[pl.BlockSpec(memory_space=pltpu.SMEM)] + [vmem] * 8,
        out_specs=[vmem] * 3,
        out_shape=[pltpu.VMEM((tile_x, 2 * snaps, tile_y), bf16), half, half],
        scratch_shapes=[
            pltpu.VMEM((256, 256), bf16),
            pltpu.VMEM((256, 128), bf16),
            pltpu.VMEM((XB, 240, 256), bf16),
            pltpu.VMEM((256, 256), f32),
        ],
        compiler_params=pltpu.CompilerParams(vmem_limit_bytes=32 * 2**20),
        name="stencil",
    )(core, rows, wide, xlow, xhigh, left, right, inv_dx, inv_dy)


def split(a):
    hi = a.astype(bf16)
    return hi, (a - hi.astype(f32)).astype(bf16)


def product(a, b):
    (ah, al), (bh, bl) = a, b
    left = jnp.concatenate([ah, ah, al], axis=1)
    right = jnp.concatenate([bh, bl, bh], axis=0)
    return jnp.dot(left, right, preferred_element_type=f32)


def rebuild_kernel(core_ref, mine_ref, other_ref, s_ref, vort_hbm, div_hbm, filt, swap, mixed, stage, sems):
    swap[...] = swap_matrix()
    first = core_ref[0] == 0
    cross = jnp.where(first, mine_ref[0:128], other_ref[0:128])
    both = jnp.where(first, other_ref[0:128], mine_ref[0:128])
    diag = jnp.where(first, other_ref[128:136], mine_ref[128:136])[0:1]
    r, c = iotas(128, 128)
    turned = both.T
    vv = jnp.where(r <= c, both, turned)
    dd = jnp.where(r == c, diag, jnp.where(r > c, both, turned))
    gram = jnp.concatenate(
        [jnp.concatenate([vv, cross], axis=1), jnp.concatenate([cross.T, dd], axis=1)], axis=0
    )
    r, c = iotas(256, 256)
    eye = jnp.where(r == c, 1.0, 0.0)
    shift = jnp.sum(gram * eye, keepdims=True) * (1.0 / 256.0)
    scale = jnp.sqrt(jnp.sum(gram * gram, keepdims=True))
    signum = (gram - shift * eye) / scale
    for _ in range(ITERS):
        parts = split(signum)
        square = product(parts, parts)
        cube = product(parts, split(square))
        signum = 1.5 * signum - 0.5 * cube
    filt[...] = ((eye + signum) * 0.5).astype(bf16)

    def chunk(i, q):
        out = vort_hbm if q < 2 else div_hbm
        return pltpu.make_async_copy(
            stage.at[i, pl.ds(64 * q, 64)],
            out.at[pl.ds(64 * (q % 2), 64), pl.ds(16 * i, 16)],
            sems.at[i, q],
        )

    for i in range(2):
        weights = filt[...]
        for k in range(16):
            mixed[i, k] = jnp.dot(weights, s_ref[16 * i + k], preferred_element_type=f32).astype(bf16)
        p = swap[...]
        for k in range(16):
            block = mixed[i, :, 16 * k : 16 * k + 16, :].reshape(256, 256)
            rows = jnp.dot(p, block, preferred_element_type=f32).astype(bf16).reshape(16, 16, 256)
            stage[i, 16 * k : 16 * k + 16] = rows
            if k % 4 == 3:
                chunk(i, k // 4).start()
    for i in range(2):
        for q in range(4):
            chunk(i, q).wait()


def rebuild(core, mine, other, s):
    tile_x, rows, tile_y = s.shape
    vmem = pl.BlockSpec(memory_space=pltpu.VMEM)
    whole = pl.BlockSpec(memory_space=pltpu.HBM)
    shape = jax.ShapeDtypeStruct((128, tile_x, tile_y), bf16)
    return pl.pallas_call(
        rebuild_kernel,
        in_specs=[pl.BlockSpec(memory_space=pltpu.SMEM), vmem, vmem, vmem],
        out_specs=[whole, whole],
        out_shape=[shape, shape],
        scratch_shapes=[
            pltpu.VMEM((256, 256), bf16),
            pltpu.VMEM((256, 256), bf16),
            pltpu.VMEM((2, 16, 256, 256), bf16),
            pltpu.VMEM((2, 256, 16, 256), bf16),
            pltpu.SemaphoreType.DMA((2, 4)),
        ],
        compiler_params=pltpu.CompilerParams(vmem_limit_bytes=32 * 2**20),
        name="rebuild",
    )(core, mine, other, s)


def moved(block, axis, target):
    return lax.ppermute(block, axis, [(i, target(i)) for i in range(lax.axis_size(axis))])


def digit(low, count, by):
    def target(i):
        at = i // low % count
        return i + ((at + by) % count - at) * low

    return target


def gathered_sum(block, axis, low, count, steps):
    others = [moved(block, axis, digit(low, count, by)) for by in steps]
    for other in others:
        block = block + other
    return block


def per_device(u_vel, v_vel, inv_dx, inv_dy):
    core = jnp.reshape(lax.axis_index("gx") & 1, (1,)).astype(jnp.int32)
    rows, wide, ends, xlow, xhigh = relayout(core, u_vel, v_vel)

    def shifted(block, axis, step):
        count = lax.axis_size(axis)
        return lax.ppermute(block, axis, [(i, i + step) for i in range(count) if 0 <= i + step < count])

    from_low = shifted(xhigh, "gx", 1)
    from_high = shifted(xlow, "gx", -1)
    from_left = shifted(ends, "gy", 1)
    from_right = shifted(ends, "gy", -1)
    s, keep, give = stencil(core, rows, wide, from_low, from_high, from_left, from_right, inv_dx, inv_dy)
    part = keep + moved(give, "gx", digit(1, 2, 1))
    part = gathered_sum(part, "gx", 2, 4, (1, 2, 3))
    part = gathered_sum(part, "gx", 8, 4, (1, 2, 3))
    for partner in (lambda z: z ^ 1, lambda z: z ^ 2, lambda z: 7 - z):
        part = part + moved(part, "gy", partner)
    other = moved(part, "gx", digit(1, 2, 1))
    return tuple(rebuild(core, part, other, s))


def solution(mesh):
    in_specs = (P(None, "gx", "gy"), P(None, "gx", "gy"), P("gx", "gy"), P("gx", "gy"))
    out_specs = (P(None, "gx", "gy"), P(None, "gx", "gy"))
    return jax.shard_map(
        per_device, mesh=mesh, in_specs=in_specs, out_specs=out_specs, check_vma=False
    )
```

```python
import functools

import jax
import jax.numpy as jnp
from jax import lax
from jax.experimental import pallas as pl
from jax.experimental.pallas import tpu as pltpu
from jax.sharding import PartitionSpec as P

ITERS = 8
TB = 16
HALF_ROWS = 136


f32 = jnp.float32
bf16 = jnp.bfloat16


def iotas(rows, cols):
    r = lax.broadcasted_iota(jnp.int32, (rows, cols), 0)
    c = lax.broadcasted_iota(jnp.int32, (rows, cols), 1)
    return r, c


def swap_matrix():
    r, c = iotas(256, 256)
    return jnp.where(c == ((r & 15) << 4) + (r >> 4), 1.0, 0.0).astype(bf16)


def relayout_kernel(core_ref, u_hbm, v_hbm, rows_ref, wide_ref, ends_ref, xlow_ref, xhigh_ref, u, v, swap, sems):
    def chunk(k, f):
        at = pl.ds(TB * k, TB)
        return pltpu.make_async_copy((u_hbm, v_hbm)[f].at[at], (u, v)[f].at[at], sems.at[k, f])

    for k in range(8):
        for f in range(2):
            chunk(k, f).start()
    swap[...] = swap_matrix()
    _, lane = iotas(TB, 128)

    @pl.loop(0, 8)
    def _(i):
        at = pl.ds(pl.multiple_of(TB * i, TB), TB)
        p = swap[...]
        for f in range(2):
            chunk(i, f).wait()
        for f, tile in enumerate((u, v)):
            ends = jnp.zeros((TB, 128), f32)
            for h in range(2):
                block = tile[at, 16 * h : 16 * h + 16, :].reshape(256, 256)
                rows = jnp.dot(p, block, preferred_element_type=f32)
                rows_ref[16 * h : 16 * h + 16, f, at] = rows.astype(bf16).reshape(16, TB, 256)
                wide_ref[16 * h : 16 * h + 16, f, at] = rows.reshape(16, TB, 256)
                for k in range(16):
                    x = 16 * h + k
                    part = rows[TB * k : TB * k + TB]
                    part = jnp.where(lane < 64, part[:, 0:128], part[:, 128:256])
                    part = pltpu.roll(part, (4 * x + 2) % 128, axis=1)
                    ends = jnp.where((lane >> 2) == x, part, ends)
            ends_ref[at, 128 * f : 128 * f + 128] = ends.astype(bf16)

    for k in range(2):
        xlow_ref[k] = rows_ref[k]
        xhigh_ref[k] = rows_ref[30 + k]


def relayout(core, u, v):
    snaps, tile_x, tile_y = u.shape
    vmem = pl.BlockSpec(memory_space=pltpu.VMEM)
    whole = pl.BlockSpec(memory_space=pltpu.HBM)
    return pl.pallas_call(
        relayout_kernel,
        in_specs=[pl.BlockSpec(memory_space=pltpu.SMEM), whole, whole],
        out_specs=[vmem] * 5,
        out_shape=[
            pltpu.VMEM((tile_x, 2, snaps, tile_y), bf16),
            pltpu.VMEM((tile_x, 2, snaps, tile_y), f32),
            pltpu.VMEM((snaps, 256), bf16),
            pltpu.VMEM((2, 2, snaps, tile_y), bf16),
            pltpu.VMEM((2, 2, snaps, tile_y), bf16),
        ],
        scratch_shapes=[
            pltpu.VMEM((snaps, tile_x, tile_y), bf16),
            pltpu.VMEM((snaps, tile_x, tile_y), bf16),
            pltpu.VMEM((256, 256), bf16),
            pltpu.SemaphoreType.DMA((8, 2)),
        ],
        compiler_params=pltpu.CompilerParams(vmem_limit_bytes=50 * 2**20),
        name="relayout",
    )(core, u, v)


XB = 4


def stencil_kernel(
    core_ref, rows_ref, wide_ref, xlow_ref, xhigh_ref, left_ref, right_ref, idx_ref, idy_ref,
    s_ref, keep_ref, give_ref,
    band, ends, tall, gram,
):
    r, c = iotas(256, 256)
    d = c - r
    band[...] = (
        jnp.where(d == 2, 1.0, 0.0) - jnp.where(d == 1, 8.0, 0.0)
        + jnp.where(d == -1, 8.0, 0.0) - jnp.where(d == -2, 1.0, 0.0)
    ).astype(bf16)
    _, lane = iotas(128, 128)
    for f in range(2):
        at = slice(128 * f, 128 * f + 128)
        ends[at] = jnp.where(
            (lane & 3) < 2, left_ref[:, at].astype(f32), right_ref[:, at].astype(f32)
        ).astype(bf16)
    r, c = iotas(240, 256)
    for j in range(XB):
        m = r - (112 + 4 * j)
        tall[j] = (
            jnp.where(((m == 0) & (c == 0)) | ((m == 1) & (c == 1)), 1.0, 0.0)
            - jnp.where((m == 1) & (c == 0), 8.0, 0.0)
            + jnp.where((m == 2) & (c == 255), 8.0, 0.0)
            - jnp.where(((m == 2) & (c == 254)) | ((m == 3) & (c == 255)), 1.0, 0.0)
        ).astype(bf16)
    gram[...] = jnp.zeros_like(gram)

    def wide(x):
        if isinstance(x, int) and x < 0:
            return xlow_ref[x + 2].reshape(256, 256).astype(f32)
        if isinstance(x, int) and x >= 32:
            return xhigh_ref[x - 32].reshape(256, 256).astype(f32)
        return wide_ref[x].reshape(256, 256)

    def group(g):
        parts = []
        start = 112 - 16 * g
        if not isinstance(g, int):
            start = pl.multiple_of(start, 16)
        for j in range(XB):
            x = XB * g + j
            dy = jnp.dot(
                jnp.concatenate([rows_ref[x].reshape(256, 256), ends[...]], axis=1),
                jnp.concatenate([band[...], tall[j, pl.ds(start, 128)]], axis=0),
                preferred_element_type=f32,
            )
            dx = 8.0 * (wide(x + 1) - wide(x - 1)) + (wide(x - 2) - wide(x + 2))
            inv_x = idx_ref[pl.ds(x, 1), :] * (1.0 / 12.0)
            inv_y = idy_ref[pl.ds(x, 1), :] * (1.0 / 12.0)
            vort = (inv_x * dx[128:256] - inv_y * dy[0:128]).astype(bf16)
            div = (inv_x * dx[0:128] + inv_y * dy[128:256]).astype(bf16)
            both = jnp.concatenate([vort, div], axis=0)
            s_ref[x] = both
            parts.append(both)
        cells = jnp.concatenate(parts, axis=1)
        gram[...] += lax.dot_general(
            cells, cells, (((1,), (1,)), ((), ())), preferred_element_type=f32
        )

    group(0)

    @pl.loop(1, 7)
    def _(g):
        group(g)

    group(7)

    r, c = iotas(128, 128)
    dd = gram[128:256, 128:256]
    mixed = jnp.where(r <= c, gram[0:128, 0:128], dd)
    diag = jnp.sum(jnp.where(r == c, dd, 0.0), axis=0, keepdims=True)
    diag = jnp.broadcast_to(diag, (8, 128))
    first = core_ref[0] == 0
    cross = gram[0:128, 128:256]
    keep_ref[0:128] = jnp.where(first, cross, mixed)
    give_ref[0:128] = jnp.where(first, mixed, cross)
    keep_ref[128:136] = jnp.where(first, 0.0, diag)
    give_ref[128:136] = jnp.where(first, diag, 0.0)


def stencil(core, rows, wide, xlow, xhigh, left, right, inv_dx, inv_dy):
    tile_x, _, snaps, tile_y = rows.shape
    vmem = pl.BlockSpec(memory_space=pltpu.VMEM)
    half = pltpu.VMEM((HALF_ROWS, 128), f32)
    return pl.pallas_call(
        stencil_kernel,
        in_specs=[pl.BlockSpec(memory_space=pltpu.SMEM)] + [vmem] * 8,
        out_specs=[vmem] * 3,
        out_shape=[pltpu.VMEM((tile_x, 2 * snaps, tile_y), bf16), half, half],
        scratch_shapes=[
            pltpu.VMEM((256, 256), bf16),
            pltpu.VMEM((256, 128), bf16),
            pltpu.VMEM((XB, 240, 256), bf16),
            pltpu.VMEM((256, 256), f32),
        ],
        compiler_params=pltpu.CompilerParams(vmem_limit_bytes=32 * 2**20),
        name="stencil",
    )(core, rows, wide, xlow, xhigh, left, right, inv_dx, inv_dy)


def split(a):
    hi = a.astype(bf16)
    return hi, (a - hi.astype(f32)).astype(bf16)


def product(a, b):
    (ah, al), (bh, bl) = a, b
    left = jnp.concatenate([ah, ah, al], axis=1)
    right = jnp.concatenate([bh, bl, bh], axis=0)
    return jnp.dot(left, right, preferred_element_type=f32)


def rebuild_kernel(core_ref, mine_ref, other_ref, s_ref, vort_hbm, div_hbm, filt, swap, mixed, stage, sems):
    swap[...] = swap_matrix()
    first = core_ref[0] == 0
    cross = jnp.where(first, mine_ref[0:128], other_ref[0:128])
    both = jnp.where(first, other_ref[0:128], mine_ref[0:128])
    diag = jnp.where(first, other_ref[128:136], mine_ref[128:136])[0:1]
    r, c = iotas(128, 128)
    turned = both.T
    vv = jnp.where(r <= c, both, turned)
    dd = jnp.where(r == c, diag, jnp.where(r > c, both, turned))
    gram = jnp.concatenate(
        [jnp.concatenate([vv, cross], axis=1), jnp.concatenate([cross.T, dd], axis=1)], axis=0
    )
    r, c = iotas(256, 256)
    eye = jnp.where(r == c, 1.0, 0.0)
    shift = jnp.sum(gram * eye, keepdims=True) * (1.0 / 256.0)
    scale = jnp.sqrt(jnp.sum(gram * gram, keepdims=True))
    signum = (gram - shift * eye) / scale
    for _ in range(ITERS):
        parts = split(signum)
        square = product(parts, parts)
        cube = product(split(square), parts)
        signum = 1.5 * signum - 0.5 * cube
    filt[...] = ((eye + signum) * 0.5).astype(bf16)

    def chunk(i, q):
        out = vort_hbm if q < 2 else div_hbm
        return pltpu.make_async_copy(
            stage.at[i, pl.ds(64 * q, 64)],
            out.at[pl.ds(64 * (q % 2), 64), pl.ds(16 * i, 16)],
            sems.at[i, q],
        )

    for i in range(2):
        weights = filt[...]
        for k in range(16):
            mixed[i, k] = jnp.dot(weights, s_ref[16 * i + k], preferred_element_type=f32).astype(bf16)
        p = swap[...]
        for k in range(16):
            block = mixed[i, :, 16 * k : 16 * k + 16, :].reshape(256, 256)
            rows = jnp.dot(p, block, preferred_element_type=f32).astype(bf16).reshape(16, 16, 256)
            stage[i, 16 * k : 16 * k + 16] = rows
            if k % 4 == 3:
                chunk(i, k // 4).start()
    for i in range(2):
        for q in range(4):
            chunk(i, q).wait()


def rebuild(core, mine, other, s):
    tile_x, rows, tile_y = s.shape
    vmem = pl.BlockSpec(memory_space=pltpu.VMEM)
    whole = pl.BlockSpec(memory_space=pltpu.HBM)
    shape = jax.ShapeDtypeStruct((128, tile_x, tile_y), bf16)
    return pl.pallas_call(
        rebuild_kernel,
        in_specs=[pl.BlockSpec(memory_space=pltpu.SMEM), vmem, vmem, vmem],
        out_specs=[whole, whole],
        out_shape=[shape, shape],
        scratch_shapes=[
            pltpu.VMEM((256, 256), bf16),
            pltpu.VMEM((256, 256), bf16),
            pltpu.VMEM((2, 16, 256, 256), bf16),
            pltpu.VMEM((2, 256, 16, 256), bf16),
            pltpu.SemaphoreType.DMA((2, 4)),
        ],
        compiler_params=pltpu.CompilerParams(vmem_limit_bytes=32 * 2**20),
        name="rebuild",
    )(core, mine, other, s)


def moved(block, axis, target):
    return lax.ppermute(block, axis, [(i, target(i)) for i in range(lax.axis_size(axis))])


def digit(low, count, by):
    def target(i):
        at = i // low % count
        return i + ((at + by) % count - at) * low

    return target


def gathered_sum(block, axis, low, count, steps):
    others = [moved(block, axis, digit(low, count, by)) for by in steps]
    for other in others:
        block = block + other
    return block


def per_device(u_vel, v_vel, inv_dx, inv_dy):
    core = jnp.reshape(lax.axis_index("gx") & 1, (1,)).astype(jnp.int32)
    rows, wide, ends, xlow, xhigh = relayout(core, u_vel, v_vel)

    def shifted(block, axis, step):
        count = lax.axis_size(axis)
        return lax.ppermute(block, axis, [(i, i + step) for i in range(count) if 0 <= i + step < count])

    from_low = shifted(xhigh, "gx", 1)
    from_high = shifted(xlow, "gx", -1)
    from_left = shifted(ends, "gy", 1)
    from_right = shifted(ends, "gy", -1)
    s, keep, give = stencil(core, rows, wide, from_low, from_high, from_left, from_right, inv_dx, inv_dy)
    part = keep + moved(give, "gx", digit(1, 2, 1))
    part = gathered_sum(part, "gx", 2, 4, (1, 2, 3))
    part = gathered_sum(part, "gx", 8, 4, (1, 2, 3))
    for partner in (lambda z: z ^ 1, lambda z: z ^ 2, lambda z: 7 - z):
        part = part + moved(part, "gy", partner)
    other = moved(part, "gx", digit(1, 2, 1))
    return tuple(rebuild(core, part, other, s))


def solution(mesh):
    in_specs = (P(None, "gx", "gy"), P(None, "gx", "gy"), P("gx", "gy"), P("gx", "gy"))
    out_specs = (P(None, "gx", "gy"), P(None, "gx", "gy"))
    return jax.shard_map(
        per_device, mesh=mesh, in_specs=in_specs, out_specs=out_specs, check_vma=False
    )
```

```python
import functools

import jax
import jax.numpy as jnp
from jax import lax
from jax.experimental import pallas as pl
from jax.experimental.pallas import tpu as pltpu
from jax.sharding import PartitionSpec as P

ITERS = 8
TB = 16
HALF_ROWS = 136


f32 = jnp.float32
bf16 = jnp.bfloat16


def iotas(rows, cols):
    r = lax.broadcasted_iota(jnp.int32, (rows, cols), 0)
    c = lax.broadcasted_iota(jnp.int32, (rows, cols), 1)
    return r, c


def swap_matrix():
    r, c = iotas(256, 256)
    return jnp.where(c == ((r & 15) << 4) + (r >> 4), 1.0, 0.0).astype(bf16)


def relayout_kernel(core_ref, u_hbm, v_hbm, rows_ref, wide_ref, ends_ref, xlow_ref, xhigh_ref, u, v, swap, sems):
    def chunk(k, f):
        at = pl.ds(TB * k, TB)
        return pltpu.make_async_copy((u_hbm, v_hbm)[f].at[at], (u, v)[f].at[at], sems.at[k, f])

    for k in range(8):
        for f in range(2):
            chunk(k, f).start()
    swap[...] = swap_matrix()
    _, lane = iotas(TB, 128)

    @pl.loop(0, 8)
    def _(i):
        at = pl.ds(pl.multiple_of(TB * i, TB), TB)
        p = swap[...]
        for f in range(2):
            chunk(i, f).wait()
        for f, tile in enumerate((u, v)):
            ends = jnp.zeros((TB, 128), f32)
            for h in range(2):
                block = tile[at, 16 * h : 16 * h + 16, :].reshape(256, 256)
                rows = jnp.dot(p, block, preferred_element_type=f32)
                rows_ref[16 * h : 16 * h + 16, f, at] = rows.astype(bf16).reshape(16, TB, 256)
                wide_ref[16 * h : 16 * h + 16, f, at] = rows.reshape(16, TB, 256)
                for k in range(16):
                    x = 16 * h + k
                    part = rows[TB * k : TB * k + TB]
                    part = jnp.where(lane < 64, part[:, 0:128], part[:, 128:256])
                    part = pltpu.roll(part, (4 * x + 2) % 128, axis=1)
                    ends = jnp.where((lane >> 2) == x, part, ends)
            ends_ref[at, 128 * f : 128 * f + 128] = ends.astype(bf16)

    for k in range(2):
        xlow_ref[k] = rows_ref[k]
        xhigh_ref[k] = rows_ref[30 + k]


def relayout(core, u, v):
    snaps, tile_x, tile_y = u.shape
    vmem = pl.BlockSpec(memory_space=pltpu.VMEM)
    whole = pl.BlockSpec(memory_space=pltpu.HBM)
    return pl.pallas_call(
        relayout_kernel,
        in_specs=[pl.BlockSpec(memory_space=pltpu.SMEM), whole, whole],
        out_specs=[vmem] * 5,
        out_shape=[
            pltpu.VMEM((tile_x, 2, snaps, tile_y), bf16),
            pltpu.VMEM((tile_x, 2, snaps, tile_y), f32),
            pltpu.VMEM((snaps, 256), bf16),
            pltpu.VMEM((2, 2, snaps, tile_y), bf16),
            pltpu.VMEM((2, 2, snaps, tile_y), bf16),
        ],
        scratch_shapes=[
            pltpu.VMEM((snaps, tile_x, tile_y), bf16),
            pltpu.VMEM((snaps, tile_x, tile_y), bf16),
            pltpu.VMEM((256, 256), bf16),
            pltpu.SemaphoreType.DMA((8, 2)),
        ],
        compiler_params=pltpu.CompilerParams(vmem_limit_bytes=50 * 2**20),
        name="relayout",
    )(core, u, v)


XB = 4


def stencil_kernel(
    core_ref, rows_ref, wide_ref, xlow_ref, xhigh_ref, left_ref, right_ref, idx_ref, idy_ref,
    s_ref, keep_ref, give_ref,
    band, ends, tall, gram,
):
    r, c = iotas(256, 256)
    d = c - r
    band[...] = (
        jnp.where(d == 2, 1.0, 0.0) - jnp.where(d == 1, 8.0, 0.0)
        + jnp.where(d == -1, 8.0, 0.0) - jnp.where(d == -2, 1.0, 0.0)
    ).astype(bf16)
    _, lane = iotas(128, 128)
    for f in range(2):
        at = slice(128 * f, 128 * f + 128)
        ends[at] = jnp.where(
            (lane & 3) < 2, left_ref[:, at].astype(f32), right_ref[:, at].astype(f32)
        ).astype(bf16)
    r, c = iotas(240, 256)
    for j in range(XB):
        m = r - (112 + 4 * j)
        tall[j] = (
            jnp.where(((m == 0) & (c == 0)) | ((m == 1) & (c == 1)), 1.0, 0.0)
            - jnp.where((m == 1) & (c == 0), 8.0, 0.0)
            + jnp.where((m == 2) & (c == 255), 8.0, 0.0)
            - jnp.where(((m == 2) & (c == 254)) | ((m == 3) & (c == 255)), 1.0, 0.0)
        ).astype(bf16)
    gram[...] = jnp.zeros_like(gram)

    def wide(x):
        if isinstance(x, int) and x < 0:
            return xlow_ref[x + 2].reshape(256, 256).astype(f32)
        if isinstance(x, int) and x >= 32:
            return xhigh_ref[x - 32].reshape(256, 256).astype(f32)
        return wide_ref[x].reshape(256, 256)

    def group(g):
        parts = []
        start = 112 - 16 * g
        if not isinstance(g, int):
            start = pl.multiple_of(start, 16)
        for j in range(XB):
            x = XB * g + j
            dy = jnp.dot(
                jnp.concatenate([rows_ref[x].reshape(256, 256), ends[...]], axis=1),
                jnp.concatenate([band[...], tall[j, pl.ds(start, 128)]], axis=0),
                preferred_element_type=f32,
            )
            dx = 8.0 * (wide(x + 1) - wide(x - 1)) + (wide(x - 2) - wide(x + 2))
            inv_x = idx_ref[pl.ds(x, 1), :] * (1.0 / 12.0)
            inv_y = idy_ref[pl.ds(x, 1), :] * (1.0 / 12.0)
            vort = (inv_x * dx[128:256] - inv_y * dy[0:128]).astype(bf16)
            div = (inv_x * dx[0:128] + inv_y * dy[128:256]).astype(bf16)
            both = jnp.concatenate([vort, div], axis=0)
            s_ref[x] = both
            parts.append(both)
        cells = jnp.concatenate(parts, axis=1)
        gram[...] += lax.dot_general(
            cells, cells, (((1,), (1,)), ((), ())), preferred_element_type=f32
        )

    group(0)

    @pl.loop(1, 7)
    def _(g):
        group(g)

    group(7)

    r, c = iotas(128, 128)
    dd = gram[128:256, 128:256]
    mixed = jnp.where(r <= c, gram[0:128, 0:128], dd)
    diag = jnp.sum(jnp.where(r == c, dd, 0.0), axis=0, keepdims=True)
    diag = jnp.broadcast_to(diag, (8, 128))
    first = core_ref[0] == 0
    cross = gram[0:128, 128:256]
    keep_ref[0:128] = jnp.where(first, cross, mixed)
    give_ref[0:128] = jnp.where(first, mixed, cross)
    keep_ref[128:136] = jnp.where(first, 0.0, diag)
    give_ref[128:136] = jnp.where(first, diag, 0.0)


def stencil(core, rows, wide, xlow, xhigh, left, right, inv_dx, inv_dy):
    tile_x, _, snaps, tile_y = rows.shape
    vmem = pl.BlockSpec(memory_space=pltpu.VMEM)
    half = pltpu.VMEM((HALF_ROWS, 128), f32)
    return pl.pallas_call(
        stencil_kernel,
        in_specs=[pl.BlockSpec(memory_space=pltpu.SMEM)] + [vmem] * 8,
        out_specs=[vmem] * 3,
        out_shape=[pltpu.VMEM((tile_x, 2 * snaps, tile_y), bf16), half, half],
        scratch_shapes=[
            pltpu.VMEM((256, 256), bf16),
            pltpu.VMEM((256, 128), bf16),
            pltpu.VMEM((XB, 240, 256), bf16),
            pltpu.VMEM((256, 256), f32),
        ],
        compiler_params=pltpu.CompilerParams(vmem_limit_bytes=32 * 2**20),
        name="stencil",
    )(core, rows, wide, xlow, xhigh, left, right, inv_dx, inv_dy)


def split(a):
    hi = a.astype(bf16)
    return hi, (a - hi.astype(f32)).astype(bf16)


def product(a, b):
    (ah, al), (bh, bl) = a, b
    left = jnp.concatenate([ah, ah, al], axis=1)
    right = jnp.concatenate([bh, bl, bh], axis=0)
    return jnp.dot(left, right, preferred_element_type=f32)


def rebuild_kernel(core_ref, mine_ref, other_ref, s_ref, vort_hbm, div_hbm, filt, swap, mixed, stage, sems):
    swap[...] = swap_matrix()
    first = core_ref[0] == 0
    cross = jnp.where(first, mine_ref[0:128], other_ref[0:128])
    both = jnp.where(first, other_ref[0:128], mine_ref[0:128])
    diag = jnp.where(first, other_ref[128:136], mine_ref[128:136])[0:1]
    r, c = iotas(128, 128)
    turned = both.T
    vv = jnp.where(r <= c, both, turned)
    dd = jnp.where(r == c, diag, jnp.where(r > c, both, turned))
    gram = jnp.concatenate(
        [jnp.concatenate([vv, cross], axis=1), jnp.concatenate([cross.T, dd], axis=1)], axis=0
    )
    r, c = iotas(256, 256)
    eye = jnp.where(r == c, 1.0, 0.0)
    shift = jnp.sum(gram * eye, keepdims=True) * (1.0 / 256.0)
    scale = jnp.sqrt(jnp.sum(gram * gram, keepdims=True))
    signum = (gram - shift * eye) / scale
    for _ in range(ITERS):
        parts = split(signum)
        blocks = []
        for b in range(2):
            at = slice(128 * b, 128 * b + 128)
            square = product((parts[0][at], parts[1][at]), parts)
            cube = product(split(square), parts)
            blocks.append(1.5 * signum[at] - 0.5 * cube)
        signum = jnp.concatenate(blocks, axis=0)
    filt[...] = ((eye + signum) * 0.5).astype(bf16)

    def chunk(i, q):
        out = vort_hbm if q < 2 else div_hbm
        return pltpu.make_async_copy(
            stage.at[i, pl.ds(64 * q, 64)],
            out.at[pl.ds(64 * (q % 2), 64), pl.ds(16 * i, 16)],
            sems.at[i, q],
        )

    for i in range(2):
        weights = filt[...]
        for k in range(16):
            mixed[i, k] = jnp.dot(weights, s_ref[16 * i + k], preferred_element_type=f32).astype(bf16)
        p = swap[...]
        for k in range(16):
            block = mixed[i, :, 16 * k : 16 * k + 16, :].reshape(256, 256)
            rows = jnp.dot(p, block, preferred_element_type=f32).astype(bf16).reshape(16, 16, 256)
            stage[i, 16 * k : 16 * k + 16] = rows
            if k % 4 == 3:
                chunk(i, k // 4).start()
    for i in range(2):
        for q in range(4):
            chunk(i, q).wait()


def rebuild(core, mine, other, s):
    tile_x, rows, tile_y = s.shape
    vmem = pl.BlockSpec(memory_space=pltpu.VMEM)
    whole = pl.BlockSpec(memory_space=pltpu.HBM)
    shape = jax.ShapeDtypeStruct((128, tile_x, tile_y), bf16)
    return pl.pallas_call(
        rebuild_kernel,
        in_specs=[pl.BlockSpec(memory_space=pltpu.SMEM), vmem, vmem, vmem],
        out_specs=[whole, whole],
        out_shape=[shape, shape],
        scratch_shapes=[
            pltpu.VMEM((256, 256), bf16),
            pltpu.VMEM((256, 256), bf16),
            pltpu.VMEM((2, 16, 256, 256), bf16),
            pltpu.VMEM((2, 256, 16, 256), bf16),
            pltpu.SemaphoreType.DMA((2, 4)),
        ],
        compiler_params=pltpu.CompilerParams(vmem_limit_bytes=32 * 2**20),
        name="rebuild",
    )(core, mine, other, s)


def moved(block, axis, target):
    return lax.ppermute(block, axis, [(i, target(i)) for i in range(lax.axis_size(axis))])


def digit(low, count, by):
    def target(i):
        at = i // low % count
        return i + ((at + by) % count - at) * low

    return target


def gathered_sum(block, axis, low, count, steps):
    others = [moved(block, axis, digit(low, count, by)) for by in steps]
    for other in others:
        block = block + other
    return block


def per_device(u_vel, v_vel, inv_dx, inv_dy):
    core = jnp.reshape(lax.axis_index("gx") & 1, (1,)).astype(jnp.int32)
    rows, wide, ends, xlow, xhigh = relayout(core, u_vel, v_vel)

    def shifted(block, axis, step):
        count = lax.axis_size(axis)
        return lax.ppermute(block, axis, [(i, i + step) for i in range(count) if 0 <= i + step < count])

    from_low = shifted(xhigh, "gx", 1)
    from_high = shifted(xlow, "gx", -1)
    from_left = shifted(ends, "gy", 1)
    from_right = shifted(ends, "gy", -1)
    s, keep, give = stencil(core, rows, wide, from_low, from_high, from_left, from_right, inv_dx, inv_dy)
    part = keep + moved(give, "gx", digit(1, 2, 1))
    part = gathered_sum(part, "gx", 2, 4, (1, 2, 3))
    part = gathered_sum(part, "gx", 8, 4, (1, 2, 3))
    for partner in (lambda z: z ^ 1, lambda z: z ^ 2, lambda z: 7 - z):
        part = part + moved(part, "gy", partner)
    other = moved(part, "gx", digit(1, 2, 1))
    return tuple(rebuild(core, part, other, s))


def solution(mesh):
    in_specs = (P(None, "gx", "gy"), P(None, "gx", "gy"), P("gx", "gy"), P("gx", "gy"))
    out_specs = (P(None, "gx", "gy"), P(None, "gx", "gy"))
    return jax.shard_map(
        per_device, mesh=mesh, in_specs=in_specs, out_specs=out_specs, check_vma=False
    )
```

```python
import functools

import jax
import jax.numpy as jnp
from jax import lax
from jax.experimental import pallas as pl
from jax.experimental.pallas import tpu as pltpu
from jax.sharding import PartitionSpec as P

ITERS = 8
TB = 16
HALF_ROWS = 136


f32 = jnp.float32
bf16 = jnp.bfloat16


def iotas(rows, cols):
    r = lax.broadcasted_iota(jnp.int32, (rows, cols), 0)
    c = lax.broadcasted_iota(jnp.int32, (rows, cols), 1)
    return r, c


def swap_matrix():
    r, c = iotas(256, 256)
    return jnp.where(c == ((r & 15) << 4) + (r >> 4), 1.0, 0.0).astype(bf16)


def relayout_kernel(core_ref, u_hbm, v_hbm, rows_ref, wide_ref, ends_ref, xlow_ref, xhigh_ref, u, v, swap, sems):
    def chunk(k, f):
        at = pl.ds(TB * k, TB)
        return pltpu.make_async_copy((u_hbm, v_hbm)[f].at[at], (u, v)[f].at[at], sems.at[k, f])

    for k in range(8):
        for f in range(2):
            chunk(k, f).start()
    swap[...] = swap_matrix()
    _, lane = iotas(TB, 128)

    @pl.loop(0, 8)
    def _(i):
        at = pl.ds(pl.multiple_of(TB * i, TB), TB)
        p = swap[...]
        for f in range(2):
            chunk(i, f).wait()
        for f, tile in enumerate((u, v)):
            ends = jnp.zeros((TB, 128), f32)
            for h in range(2):
                block = tile[at, 16 * h : 16 * h + 16, :].reshape(256, 256)
                rows = jnp.dot(p, block, preferred_element_type=f32)
                rows_ref[16 * h : 16 * h + 16, f, at] = rows.astype(bf16).reshape(16, TB, 256)
                wide_ref[16 * h : 16 * h + 16, f, at] = rows.reshape(16, TB, 256)
                for k in range(16):
                    x = 16 * h + k
                    part = rows[TB * k : TB * k + TB]
                    part = jnp.where(lane < 64, part[:, 0:128], part[:, 128:256])
                    part = pltpu.roll(part, (4 * x + 2) % 128, axis=1)
                    ends = jnp.where((lane >> 2) == x, part, ends)
            ends_ref[at, 128 * f : 128 * f + 128] = ends.astype(bf16)

    for k in range(2):
        xlow_ref[k] = rows_ref[k]
        xhigh_ref[k] = rows_ref[30 + k]


def relayout(core, u, v):
    snaps, tile_x, tile_y = u.shape
    vmem = pl.BlockSpec(memory_space=pltpu.VMEM)
    whole = pl.BlockSpec(memory_space=pltpu.HBM)
    return pl.pallas_call(
        relayout_kernel,
        in_specs=[pl.BlockSpec(memory_space=pltpu.SMEM), whole, whole],
        out_specs=[vmem] * 5,
        out_shape=[
            pltpu.VMEM((tile_x, 2, snaps, tile_y), bf16),
            pltpu.VMEM((tile_x, 2, snaps, tile_y), f32),
            pltpu.VMEM((snaps, 256), bf16),
            pltpu.VMEM((2, 2, snaps, tile_y), bf16),
            pltpu.VMEM((2, 2, snaps, tile_y), bf16),
        ],
        scratch_shapes=[
            pltpu.VMEM((snaps, tile_x, tile_y), bf16),
            pltpu.VMEM((snaps, tile_x, tile_y), bf16),
            pltpu.VMEM((256, 256), bf16),
            pltpu.SemaphoreType.DMA((8, 2)),
        ],
        compiler_params=pltpu.CompilerParams(vmem_limit_bytes=50 * 2**20),
        name="relayout",
    )(core, u, v)


XB = 4


def stencil_kernel(
    core_ref, rows_ref, wide_ref, xlow_ref, xhigh_ref, left_ref, right_ref, idx_ref, idy_ref,
    s_ref, keep_ref, give_ref,
    band, ends, tall, gram,
):
    r, c = iotas(256, 256)
    d = c - r
    band[...] = (
        jnp.where(d == 2, 1.0, 0.0) - jnp.where(d == 1, 8.0, 0.0)
        + jnp.where(d == -1, 8.0, 0.0) - jnp.where(d == -2, 1.0, 0.0)
    ).astype(bf16)
    _, lane = iotas(128, 128)
    for f in range(2):
        at = slice(128 * f, 128 * f + 128)
        ends[at] = jnp.where(
            (lane & 3) < 2, left_ref[:, at].astype(f32), right_ref[:, at].astype(f32)
        ).astype(bf16)
    r, c = iotas(240, 256)
    for j in range(XB):
        m = r - (112 + 4 * j)
        tall[j] = (
            jnp.where(((m == 0) & (c == 0)) | ((m == 1) & (c == 1)), 1.0, 0.0)
            - jnp.where((m == 1) & (c == 0), 8.0, 0.0)
            + jnp.where((m == 2) & (c == 255), 8.0, 0.0)
            - jnp.where(((m == 2) & (c == 254)) | ((m == 3) & (c == 255)), 1.0, 0.0)
        ).astype(bf16)
    gram[...] = jnp.zeros_like(gram)

    def wide(x):
        if isinstance(x, int) and x < 0:
            return xlow_ref[x + 2].reshape(256, 256).astype(f32)
        if isinstance(x, int) and x >= 32:
            return xhigh_ref[x - 32].reshape(256, 256).astype(f32)
        return wide_ref[x].reshape(256, 256)

    def group(g):
        parts = []
        start = 112 - 16 * g
        if not isinstance(g, int):
            start = pl.multiple_of(start, 16)
        for j in range(XB):
            x = XB * g + j
            dy = jnp.dot(
                jnp.concatenate([rows_ref[x].reshape(256, 256), ends[...]], axis=1),
                jnp.concatenate([band[...], tall[j, pl.ds(start, 128)]], axis=0),
                preferred_element_type=f32,
            )
            dx = 8.0 * (wide(x + 1) - wide(x - 1)) + (wide(x - 2) - wide(x + 2))
            inv_x = idx_ref[pl.ds(x, 1), :] * (1.0 / 12.0)
            inv_y = idy_ref[pl.ds(x, 1), :] * (1.0 / 12.0)
            vort = (inv_x * dx[128:256] - inv_y * dy[0:128]).astype(bf16)
            div = (inv_x * dx[0:128] + inv_y * dy[128:256]).astype(bf16)
            both = jnp.concatenate([vort, div], axis=0)
            s_ref[x] = both
            parts.append(both)
        cells = jnp.concatenate(parts, axis=1)
        gram[...] += lax.dot_general(
            cells, cells, (((1,), (1,)), ((), ())), preferred_element_type=f32
        )

    group(0)

    @pl.loop(1, 7, unroll=2)
    def _(g):
        group(g)

    group(7)

    r, c = iotas(128, 128)
    dd = gram[128:256, 128:256]
    mixed = jnp.where(r <= c, gram[0:128, 0:128], dd)
    diag = jnp.sum(jnp.where(r == c, dd, 0.0), axis=0, keepdims=True)
    diag = jnp.broadcast_to(diag, (8, 128))
    first = core_ref[0] == 0
    cross = gram[0:128, 128:256]
    keep_ref[0:128] = jnp.where(first, cross, mixed)
    give_ref[0:128] = jnp.where(first, mixed, cross)
    keep_ref[128:136] = jnp.where(first, 0.0, diag)
    give_ref[128:136] = jnp.where(first, diag, 0.0)


def stencil(core, rows, wide, xlow, xhigh, left, right, inv_dx, inv_dy):
    tile_x, _, snaps, tile_y = rows.shape
    vmem = pl.BlockSpec(memory_space=pltpu.VMEM)
    half = pltpu.VMEM((HALF_ROWS, 128), f32)
    return pl.pallas_call(
        stencil_kernel,
        in_specs=[pl.BlockSpec(memory_space=pltpu.SMEM)] + [vmem] * 8,
        out_specs=[vmem] * 3,
        out_shape=[pltpu.VMEM((tile_x, 2 * snaps, tile_y), bf16), half, half],
        scratch_shapes=[
            pltpu.VMEM((256, 256), bf16),
            pltpu.VMEM((256, 128), bf16),
            pltpu.VMEM((XB, 240, 256), bf16),
            pltpu.VMEM((256, 256), f32),
        ],
        compiler_params=pltpu.CompilerParams(vmem_limit_bytes=32 * 2**20),
        name="stencil",
    )(core, rows, wide, xlow, xhigh, left, right, inv_dx, inv_dy)


def split(a):
    hi = a.astype(bf16)
    return hi, (a - hi.astype(f32)).astype(bf16)


def product(a, b):
    (ah, al), (bh, bl) = a, b
    left = jnp.concatenate([ah, ah, al], axis=1)
    right = jnp.concatenate([bh, bl, bh], axis=0)
    return jnp.dot(left, right, preferred_element_type=f32)


def rebuild_kernel(core_ref, mine_ref, other_ref, s_ref, vort_hbm, div_hbm, filt, swap, mixed, stage, sems):
    swap[...] = swap_matrix()
    first = core_ref[0] == 0
    cross = jnp.where(first, mine_ref[0:128], other_ref[0:128])
    both = jnp.where(first, other_ref[0:128], mine_ref[0:128])
    diag = jnp.where(first, other_ref[128:136], mine_ref[128:136])[0:1]
    r, c = iotas(128, 128)
    turned = both.T
    vv = jnp.where(r <= c, both, turned)
    dd = jnp.where(r == c, diag, jnp.where(r > c, both, turned))
    gram = jnp.concatenate(
        [jnp.concatenate([vv, cross], axis=1), jnp.concatenate([cross.T, dd], axis=1)], axis=0
    )
    r, c = iotas(256, 256)
    eye = jnp.where(r == c, 1.0, 0.0)
    shift = jnp.sum(gram * eye, keepdims=True) * (1.0 / 256.0)
    scale = jnp.sqrt(jnp.sum(gram * gram, keepdims=True))
    signum = (gram - shift * eye) / scale
    for _ in range(ITERS):
        parts = split(signum)
        blocks = []
        for b in range(2):
            at = slice(128 * b, 128 * b + 128)
            square = product((parts[0][at], parts[1][at]), parts)
            cube = product(split(square), parts)
            blocks.append(1.5 * signum[at] - 0.5 * cube)
        signum = jnp.concatenate(blocks, axis=0)
    filt[...] = ((eye + signum) * 0.5).astype(bf16)

    def chunk(i, q):
        out = vort_hbm if q < 2 else div_hbm
        return pltpu.make_async_copy(
            stage.at[i, pl.ds(64 * q, 64)],
            out.at[pl.ds(64 * (q % 2), 64), pl.ds(16 * i, 16)],
            sems.at[i, q],
        )

    for i in range(2):
        weights = filt[...]
        for k in range(16):
            mixed[i, k] = jnp.dot(weights, s_ref[16 * i + k], preferred_element_type=f32).astype(bf16)
        p = swap[...]
        for k in range(16):
            block = mixed[i, :, 16 * k : 16 * k + 16, :].reshape(256, 256)
            rows = jnp.dot(p, block, preferred_element_type=f32).astype(bf16).reshape(16, 16, 256)
            stage[i, 16 * k : 16 * k + 16] = rows
            if k % 4 == 3:
                chunk(i, k // 4).start()
    for i in range(2):
        for q in range(4):
            chunk(i, q).wait()


def rebuild(core, mine, other, s):
    tile_x, rows, tile_y = s.shape
    vmem = pl.BlockSpec(memory_space=pltpu.VMEM)
    whole = pl.BlockSpec(memory_space=pltpu.HBM)
    shape = jax.ShapeDtypeStruct((128, tile_x, tile_y), bf16)
    return pl.pallas_call(
        rebuild_kernel,
        in_specs=[pl.BlockSpec(memory_space=pltpu.SMEM), vmem, vmem, vmem],
        out_specs=[whole, whole],
        out_shape=[shape, shape],
        scratch_shapes=[
            pltpu.VMEM((256, 256), bf16),
            pltpu.VMEM((256, 256), bf16),
            pltpu.VMEM((2, 16, 256, 256), bf16),
            pltpu.VMEM((2, 256, 16, 256), bf16),
            pltpu.SemaphoreType.DMA((2, 4)),
        ],
        compiler_params=pltpu.CompilerParams(vmem_limit_bytes=32 * 2**20),
        name="rebuild",
    )(core, mine, other, s)


def moved(block, axis, target):
    return lax.ppermute(block, axis, [(i, target(i)) for i in range(lax.axis_size(axis))])


def digit(low, count, by):
    def target(i):
        at = i // low % count
        return i + ((at + by) % count - at) * low

    return target


def gathered_sum(block, axis, low, count, steps):
    others = [moved(block, axis, digit(low, count, by)) for by in steps]
    for other in others:
        block = block + other
    return block


def per_device(u_vel, v_vel, inv_dx, inv_dy):
    core = jnp.reshape(lax.axis_index("gx") & 1, (1,)).astype(jnp.int32)
    rows, wide, ends, xlow, xhigh = relayout(core, u_vel, v_vel)

    def shifted(block, axis, step):
        count = lax.axis_size(axis)
        return lax.ppermute(block, axis, [(i, i + step) for i in range(count) if 0 <= i + step < count])

    from_low = shifted(xhigh, "gx", 1)
    from_high = shifted(xlow, "gx", -1)
    from_left = shifted(ends, "gy", 1)
    from_right = shifted(ends, "gy", -1)
    s, keep, give = stencil(core, rows, wide, from_low, from_high, from_left, from_right, inv_dx, inv_dy)
    part = keep + moved(give, "gx", digit(1, 2, 1))
    part = gathered_sum(part, "gx", 2, 4, (1, 2, 3))
    part = gathered_sum(part, "gx", 8, 4, (1, 2, 3))
    for partner in (lambda z: z ^ 1, lambda z: z ^ 2, lambda z: 7 - z):
        part = part + moved(part, "gy", partner)
    other = moved(part, "gx", digit(1, 2, 1))
    return tuple(rebuild(core, part, other, s))


def solution(mesh):
    in_specs = (P(None, "gx", "gy"), P(None, "gx", "gy"), P("gx", "gy"), P("gx", "gy"))
    out_specs = (P(None, "gx", "gy"), P(None, "gx", "gy"))
    return jax.shard_map(
        per_device, mesh=mesh, in_specs=in_specs, out_specs=out_specs, check_vma=False
    )
```
